32 devices in a mesh: row: 8 (over y, x, core), col: 4 (over z).
Axes of the slice: x: 2, y: 2, z: 4, core: 2. Of those that a mesh axis runs over, the one named last changes fastest.
Arguments:
- skew_matrix: float32 [16384, 16384], P('row', 'col'), may hold values from -80 to 80, as said below
- first_reflector: float32 [16384, 128], P('row'), may hold values from -0.05625 to 0.05625
- first_factor: float32 [128, 128], replicated, may hold values from -0.6 to 1.5, as said below
- second_reflector: float32 [16384, 128], P('row'), may hold values from -0.05625 to 0.05625
- second_factor: float32 [128, 128], replicated, may hold values from -0.6 to 1.5, as said below
- vectors: float32 [16384, 4096], P('row', 'col'), may hold values from -6 to 6
Outputs:
- updated_matrix: float32 [16384, 16384], P('row', 'col')
- back_vectors: float32 [16384, 4096], P('row', 'col')
The draws below stay inside these ranges and needn't reach their ends.
Inputs may be any that keep to these rules, and one draw needn't show every extreme that they name: skew_matrix is skew-symmetric: entry (i, j) equals minus entry (j, i) exactly. first_factor is upper triangular with a positive diagonal. second_factor is upper triangular with a positive diagonal.
All inputs are finite; a program needn't handle non-finite values.
Results may differ from the reference program's by a relative error of at most 0.000059.
Values sent between devices are 32-bit elements; how exact they have to be, the bound alone decides.
A program may use at most 192 MiB of HBM per device.

```python
import jax
import jax.numpy as jnp
from jax import lax

N = 16384
NB = 128
K = 4096


def draw_skew_matrix(key, part):
    mkey = jax.random.fold_in(key, 3)
    base = jnp.clip(jax.random.normal(mkey, (N, N), jnp.float32), -6.0, 6.0)
    skew = (base - base.T) * 0.7071
    return skew


def factor_draw(key):
    diagonal = jax.random.uniform(jax.random.fold_in(key, 1), (NB,), jnp.float32, 0.5, 1.5)
    upper = jnp.clip(0.1 * jax.random.normal(jax.random.fold_in(key, 2), (NB, NB), jnp.float32), -0.6, 0.6)
    return jnp.triu(upper, 1) + jnp.diag(diagonal)


def draw_first_factor(key, part):
    return factor_draw(jax.random.fold_in(key, 11))


def draw_second_factor(key, part):
    return factor_draw(jax.random.fold_in(key, 12))


def level_of(stream_key, extent, cuts, smallest, high):
    loudness = 1.0
    for position, blocks in cuts:
        heights = jax.random.uniform(jax.random.fold_in(jax.random.fold_in(stream_key, 6), position), (blocks,), jnp.float32, smallest / len(cuts), high / len(cuts))
        loudness = loudness * jnp.repeat(jnp.exp(heights), extent[position] // blocks).reshape((-1,) + (1,) * (len(extent) - 1 - position))
    return loudness


def centred(stream_key, shape, scale, limit, cuts=(), held_as=jnp.bfloat16):
    entries = jax.random.normal(stream_key, shape, jnp.float32) * scale
    if len(cuts) > 0:
        entries = level_of(stream_key, shape, cuts, -0.22, 0.18) * entries
    return jnp.clip(entries, min=-limit, max=limit).astype(held_as)


def setup_inputs(seed: int = 0) -> dict:
    keys = jax.random.split(jax.random.key(seed), 7)
    return {
        "skew_matrix": draw_skew_matrix(jax.random.fold_in(keys[6], 71), 0),
        "first_reflector": centred(keys[1], (N, NB), (1.2 / N**0.5), 0.05625, ((0, 8),), jnp.float32),
        "first_factor": draw_first_factor(jax.random.fold_in(keys[6], 71), 0),
        "second_reflector": centred(keys[3], (N, NB), (1.2 / N**0.5), 0.05625, ((0, 8),), jnp.float32),
        "second_factor": draw_second_factor(jax.random.fold_in(keys[6], 71), 0),
        "vectors": centred(keys[5], (N, K), 1.0, 6.0, ((0, 8), (1, 4)), jnp.float32),
    }


def multiply(left, right):
    return jnp.dot(left, right, precision=lax.Precision.HIGHEST, preferred_element_type=jnp.float32)


def transform(matrix, reflector, factor):
    product = multiply(matrix, reflector)
    wide = multiply(product, factor)
    gram = multiply(reflector.T, product)
    correction = multiply(multiply(factor.T, gram), factor)
    fixed = wide - 0.5 * multiply(reflector, correction)
    left = jnp.concatenate([reflector, -fixed], axis=1)
    right = jnp.concatenate([fixed, reflector], axis=1)
    return matrix + multiply(left, right.T)


def back_apply(vectors, reflector, factor):
    sums = multiply(reflector.T, vectors)
    return vectors - multiply(reflector, multiply(factor, sums))


def reference(skew_matrix, first_reflector, first_factor, second_reflector, second_factor, vectors):
    inner = transform(skew_matrix, first_reflector, first_factor)
    updated_matrix = transform(inner, second_reflector, second_factor)
    middle = back_apply(vectors, second_reflector, second_factor)
    back_vectors = back_apply(middle, first_reflector, first_factor)
    return updated_matrix, back_vectors
```

```python
import jax
import jax.numpy as jnp
from jax import lax
from jax.sharding import PartitionSpec as P

HIGH = lax.Precision.HIGH
FULL = lax.Precision.HIGHEST


def dot(left, right, dims, precision=HIGH):
    return lax.dot_general(
        left, right, (dims, ((), ())), precision=precision, preferred_element_type=jnp.float32
    )


NN = ((1,), (0,))
TN = ((0,), (0,))
NT = ((1,), (1,))


def panel_of(block, rows, cols):
    share = rows // cols
    length = block.shape[0]
    col = lax.axis_index("col")
    row = lax.axis_index("row")
    if rows % cols or cols & (cols - 1) or cols < 2 or share != 2:
        whole = lax.all_gather(block, "row", axis=0, tiled=True)
        width = length * rows // cols
        return lax.dynamic_slice_in_dim(whole, col * width, width, 0)
    bits = []
    bit = 1
    while bit < cols:
        bits.append(bit)
        bit *= 2
    have = (row // share) == col
    pieces = []
    half = length // 2
    for turn in range(2):
        order = bits[turn:] + bits[:turn]
        part = jnp.where(have, block[turn * half : (turn + 1) * half], 0.0)
        reached = [0]
        for bit in order:
            pairs = []
            for c in range(cols):
                for offset in reached:
                    k = c ^ offset
                    for j in range(share):
                        pairs.append(((k * share + j) * cols + c, ((k ^ bit) * share + j) * cols + c))
            part = part + lax.ppermute(part, ("row", "col"), pairs)
            reached = reached + [offset ^ bit for offset in reached]
        swap = [(r, r ^ 1) for r in range(rows)]
        other = lax.ppermute(part, "row", swap)
        pieces.append((part, other))
    first = jnp.concatenate([pieces[0][0], pieces[1][0]], axis=0)
    second = jnp.concatenate([pieces[0][1], pieces[1][1]], axis=0)
    even = (row % 2) == 0
    return jnp.concatenate([jnp.where(even, first, second), jnp.where(even, second, first)], axis=0)


def solution(mesh):
    rows, cols = mesh.shape["row"], mesh.shape["col"]

    def shards(matrix, first, factor1, second, factor2, vectors):
        nb = first.shape[1]
        joined = jnp.concatenate([first, second], axis=1)
        panel = panel_of(joined, rows, cols)
        inner, projected = lax.psum(
            (dot(joined, joined, TN, FULL), dot(joined, vectors, TN)), "row"
        )
        cross = inner[:nb, nb:]
        top_right = -dot(dot(factor1, cross, NN, FULL), factor2, NN, FULL)
        zeros = jnp.zeros_like(factor2)
        compact = jnp.concatenate(
            [jnp.concatenate([factor1, top_right], axis=1), jnp.concatenate([zeros, factor2], axis=1)],
            axis=0,
        )
        back = vectors - dot(joined, dot(compact, projected, NN), NN)

        product = lax.psum(dot(matrix, panel, NN), "col")
        product, inner, projected = lax.optimization_barrier((product, inner, projected))
        gram = lax.psum(dot(joined, product, TN), "row")
        product_panel = panel_of(product, rows, cols)

        x1 = dot(dot(factor1, gram[:nb, :nb], TN, FULL), factor1, NN, FULL)
        key = dot(factor1, gram[nb:, :nb], ((0,), (1,)), FULL) - 0.5 * dot(x1, cross, TN, FULL)
        twist = dot(cross, key, TN, FULL)
        gram2 = gram[nb:, nb:] + twist - twist.T
        x2 = dot(dot(factor2, gram2, TN, FULL), factor2, NN, FULL)
        mixed = dot(key + 0.5 * dot(x1, cross, NN, FULL), factor2, NN, FULL)
        b = jnp.concatenate(
            [jnp.concatenate([-0.5 * x1, mixed], axis=1), jnp.concatenate([zeros, -0.5 * x2], axis=1)],
            axis=0,
        )
        skew = b - b.T
        right_top = dot(compact, product_panel, ((0,), (1,))) - dot(skew, panel, NT)
        right_low = -dot(compact, panel, NT)
        left = jnp.concatenate([joined, product], axis=1)
        right = jnp.concatenate([right_top, right_low], axis=0)
        return matrix + dot(left, right, NN), back

    in_specs = (P("row", "col"), P("row", None), P(), P("row", None), P(), P("row", "col"))
    out_specs = (P("row", "col"), P("row", "col"))
    return jax.shard_map(shards, mesh=mesh, in_specs=in_specs, out_specs=out_specs, check_vma=False)
```

```python
import jax
import jax.numpy as jnp
from jax import lax
from jax.sharding import PartitionSpec as P

HIGH = lax.Precision.HIGH
FULL = lax.Precision.HIGHEST


def dot(left, right, dims, precision=HIGH):
    return lax.dot_general(
        left, right, (dims, ((), ())), precision=precision, preferred_element_type=jnp.float32
    )


NN = ((1,), (0,))
TN = ((0,), (0,))
NT = ((1,), (1,))


def panel_of(block, rows, cols):
    share = rows // cols
    length = block.shape[0]
    col = lax.axis_index("col")
    row = lax.axis_index("row")
    if rows % cols or cols & (cols - 1) or cols < 2 or share != 2:
        whole = lax.all_gather(block, "row", axis=0, tiled=True)
        width = length * rows // cols
        return lax.dynamic_slice_in_dim(whole, col * width, width, 0)
    bits = []
    bit = 1
    while bit < cols:
        bits.append(bit)
        bit *= 2
    have = (row // share) == col
    pieces = []
    half = length // 2
    for turn in range(2):
        order = bits[turn:] + bits[:turn]
        part = jnp.where(have, block[turn * half : (turn + 1) * half], 0.0)
        reached = [0]
        for bit in order:
            pairs = []
            for c in range(cols):
                for offset in reached:
                    k = c ^ offset
                    for j in range(share):
                        pairs.append(((k * share + j) * cols + c, ((k ^ bit) * share + j) * cols + c))
            part = part + lax.ppermute(part, ("row", "col"), pairs)
            reached = reached + [offset ^ bit for offset in reached]
        swap = [(r, r ^ 1) for r in range(rows)]
        other = lax.ppermute(part, "row", swap)
        pieces.append((part, other))
    first = jnp.concatenate([pieces[0][0], pieces[1][0]], axis=0)
    second = jnp.concatenate([pieces[0][1], pieces[1][1]], axis=0)
    even = (row % 2) == 0
    return jnp.concatenate([jnp.where(even, first, second), jnp.where(even, second, first)], axis=0)


def sum_all(value, rows, cols):
    total = rows * cols
    if total & (total - 1):
        return lax.psum(value, ("row", "col"))
    bit = 1
    while bit < total:
        pairs = [(device, device ^ bit) for device in range(total)]
        value = value + lax.ppermute(value, ("row", "col"), pairs)
        bit *= 2
    return value


def solution(mesh):
    rows, cols = mesh.shape["row"], mesh.shape["col"]

    def shards(matrix, first, factor1, second, factor2, vectors):
        nb = first.shape[1]
        joined = jnp.concatenate([first, second], axis=1)
        share = rows // cols
        own = (dot(joined, joined, TN, FULL), dot(joined, vectors, TN))
        own, ready = lax.optimization_barrier((own, joined))
        inner, projected = lax.psum(own, "row")
        panel = panel_of(ready, rows, cols)
        cross = inner[:nb, nb:]
        top_right = -dot(dot(factor1, cross, NN, FULL), factor2, NN, FULL)
        zeros = jnp.zeros_like(factor2)
        compact = jnp.concatenate(
            [jnp.concatenate([factor1, top_right], axis=1), jnp.concatenate([zeros, factor2], axis=1)],
            axis=0,
        )
        back = vectors - dot(joined, dot(compact, projected, NN), NN)

        partial = dot(matrix, panel, NN)
        gram = sum_all(dot(joined, partial, TN), rows, cols)
        half = partial.shape[0] // 2
        upper = lax.psum(partial[:half], "col")
        upper, rest = lax.optimization_barrier((upper, partial[half:]))
        lower = lax.psum(rest, "col")
        product = jnp.concatenate([upper, lower], axis=0)
        halves = [panel_of(part, rows, cols).reshape(share, half, -1) for part in (upper, lower)]
        product_panel = jnp.concatenate(halves, axis=1).reshape(share * 2 * half, -1)

        x1 = dot(dot(factor1, gram[:nb, :nb], TN, FULL), factor1, NN, FULL)
        key = dot(factor1, gram[nb:, :nb], ((0,), (1,)), FULL) - 0.5 * dot(x1, cross, TN, FULL)
        twist = dot(cross, key, TN, FULL)
        gram2 = gram[nb:, nb:] + twist - twist.T
        x2 = dot(dot(factor2, gram2, TN, FULL), factor2, NN, FULL)
        mixed = dot(key + 0.5 * dot(x1, cross, NN, FULL), factor2, NN, FULL)
        b = jnp.concatenate(
            [jnp.concatenate([-0.5 * x1, mixed], axis=1), jnp.concatenate([zeros, -0.5 * x2], axis=1)],
            axis=0,
        )
        skew = b - b.T
        right_top = dot(compact, product_panel, ((0,), (1,))) - dot(skew, panel, NT)
        right_low = -dot(compact, panel, NT)
        left = jnp.concatenate([joined, product], axis=1)
        right = jnp.concatenate([right_top, right_low], axis=0)
        return matrix + dot(left, right, NN), back

    in_specs = (P("row", "col"), P("row", None), P(), P("row", None), P(), P("row", "col"))
    out_specs = (P("row", "col"), P("row", "col"))
    return jax.shard_map(shards, mesh=mesh, in_specs=in_specs, out_specs=out_specs, check_vma=False)
```
